32 devices in a mesh: batch: 8 (over z, y), seq: 4 (over x, core).
Axes of the slice: x: 2, y: 2, z: 4, core: 2. Of those that a mesh axis runs over, the one named last changes fastest.
Arguments:
- forward_embed: bfloat16 [12288, 1536], P(('batch', 'seq')), parts along dimension 0, may hold values from -6 to 6
- reverse_embed: bfloat16 [12288, 1536], P(('batch', 'seq')), parts along dimension 0, may hold values from -6 to 6
- conv_weight: bfloat16 [1, 3, 1536, 1536], P(None, None, 'seq'), may hold values from -0.09375 to 0.09375
- conv_bias: float32 [1, 1536], replicated, may hold values from -0.5 to 0.5
- head_weight: bfloat16 [1536, 1024], replicated, may hold values from -0.15625 to 0.15625
- head_bias: float32 [1024], replicated, may hold values from -1 to 1
Outputs:
- averaged: bfloat16 [12288, 1024], P(('batch', 'seq')), parts along dimension 0
The draws below stay inside these ranges and needn't reach their ends.
There are 8 independent parts, one for each index of `batch`. The reference program is written for one: setup_inputs(seed, part) draws one part's arguments, and reference() takes and returns one part's arrays. A program takes and returns all parts, laid end to end along the dimension named above; an argument that names none is the same for every part. Nothing has to cross between parts.
All inputs are finite; a program needn't handle non-finite values.
Results may differ from the reference program's by a relative error of at most 0.008.
Values may be sent and summed in bfloat16 or wider, within the bound.
A program may use at most 128 MiB of HBM per device.

```python
import jax
import jax.numpy as jnp

CHANNELS = 1536
TRACKS = 1024
LAYERS = 1
BINS = 1536


def level_of(stream_key, shape, cuts, low, high):
    level, own = 1.0, jax.random.fold_in(stream_key, 6)
    for dim, shards_of in cuts:
        heights = jnp.exp(jax.random.uniform(jax.random.fold_in(own, dim), (shards_of,), jnp.float32, low / len(cuts), high / len(cuts)))
        level = level * jnp.repeat(heights, shape[dim] // shards_of).reshape([-1 if axis == dim else 1 for axis in range(len(shape))])
    return level


def normal_values(key, extent, spread, limit, cuts=(), dtype=jnp.bfloat16):
    result = spread * jax.random.normal(key, extent, jnp.float32)
    if cuts:
        result = result * level_of(key, extent, cuts, -0.22, 0.18)
    return jnp.clip(result, -limit, limit).astype(dtype)


def setup_inputs(seed: int = 0, part: int = 0) -> dict:
    streams_of = jax.random.split(jax.random.key(seed), 7)
    own_keys = jax.random.split(jax.random.fold_in(streams_of[6], part), 7)
    forward_embed = normal_values(own_keys[0], (BINS, CHANNELS), 1.0, 6.0, ((0, 4),))
    reverse_embed = normal_values(own_keys[1], (BINS, CHANNELS), 1.0, 6.0, ((0, 4),))
    conv_weight = normal_values(streams_of[2], (LAYERS, 3, CHANNELS, CHANNELS), (3 * CHANNELS) ** -0.5, 0.09375, ((2, 4),))
    conv_bias = jnp.clip(jax.random.uniform(streams_of[3], (LAYERS, CHANNELS), jnp.float32, -0.5, 0.5), -0.5, 0.5)
    head_weight = normal_values(streams_of[4], (CHANNELS, TRACKS), CHANNELS ** -0.5, 0.15625)
    head_bias = jnp.clip(jax.random.uniform(streams_of[5], (TRACKS,), jnp.float32, -1.0, 1.0), -1.0, 1.0)
    return dict(forward_embed=forward_embed, reverse_embed=reverse_embed, conv_weight=conv_weight, conv_bias=conv_bias, head_weight=head_weight, head_bias=head_bias)


def convolve(hidden, kernel, bias):
    count = hidden.shape[0]
    padded = jnp.pad(hidden, ((1, 1), (0, 0)))
    acc = jnp.zeros((count, kernel.shape[2]), jnp.float32)
    for tap in range(3):
        acc = acc + jnp.dot(padded[tap:tap + count], kernel[tap], preferred_element_type=jnp.float32)
    return jax.nn.gelu(acc + bias, approximate=False).astype(jnp.bfloat16)


def strand_tracks(embed, conv_weight, conv_bias, head_weight, head_bias):
    hidden = embed
    for layer in range(LAYERS):
        hidden = convolve(hidden, conv_weight[layer], conv_bias[layer])
    logits = jnp.dot(hidden, head_weight, preferred_element_type=jnp.float32) + head_bias
    return jax.nn.softplus(logits).astype(jnp.bfloat16)


def reference(forward_embed, reverse_embed, conv_weight, conv_bias, head_weight, head_bias):
    forward_tracks = strand_tracks(forward_embed, conv_weight, conv_bias, head_weight, head_bias)
    reverse_tracks = strand_tracks(reverse_embed, conv_weight, conv_bias, head_weight, head_bias)
    mean = 0.5 * (forward_tracks.astype(jnp.float32) + reverse_tracks[::-1].astype(jnp.float32))
    return mean.astype(jnp.bfloat16)
```

```python
import functools
import math

import jax
import jax.numpy as jnp
from jax import lax
from jax.experimental import pallas as pl
from jax.experimental.pallas import tpu as pltpu
from jax.sharding import PartitionSpec as P

MESH = pl.DeviceIdType.MESH
F32 = jnp.float32
BF16 = jnp.bfloat16
LANES = 128
WIDE = 256
SPLIT = 2
START = 2
LAG = 2
LAG2 = 2
COLORS = 4
VISIT = 12


def gelu(x):
    return (0.5 * x) * (1.0 + lax.erf(x * math.sqrt(0.5)))


def softplus(x):
    u = jnp.exp(-jnp.abs(x))
    return jnp.maximum(x, 0.0) + jnp.where(u < 1e-3, u - 0.5 * u * u, jnp.log(1.0 + u))


def kernel(
    taps, fwd_hbm, rev_hbm, w_hbm, cb_hbm, hw_hbm, hb_hbm, fwd_out, rev_out,
    embed, halo, guest, xcat, wbuf, acc, headw, logits, flip, sendt, keept, cb_ref, hb_ref,
    local_sem, halo_send, halo_recv, own_send, own_recv,
    x_send, x_recv, y_send, y_recv, z_send, z_recv, m_send, m_recv, t_send, t_recv, out_sem, guest_sem,
):
    s = lax.axis_index("seq")
    b = lax.axis_index("batch")
    core = s % 2
    far = s // 2
    mate = s + 1 - 2 * core
    across = s + 2 - 4 * far
    mirror = 3 - s
    shards = (s, mate, across, mirror)
    y = b % 2
    z = (b // 2) % 2
    yp = b + 1 - 2 * y
    zp = b + 2 - 4 * z
    cx = 2 * z + y
    cy = 2 * z + 1 - y
    cz = 2 * (1 - z) + y
    cd = 2 * (1 - z) + 1 - y
    rows, channels = embed.shape[1:]
    deep = w_hbm.shape[0]
    depth = deep // taps
    wide = WIDE
    blocks = channels // wide
    units = SPLIT * blocks
    part = deep // SPLIT
    grain = part // COLORS
    thin = wide // 2
    half = 2 * taps * depth
    tracks = hb_ref.shape[1]
    pieces = tracks // wide
    visit = guest.shape[0] - halo.shape[2]
    kept = rows - visit

    barrier = pltpu.get_barrier_semaphore()
    for peer in ({"seq": mate}, {"seq": across}, {"seq": mirror}, {"batch": yp}, {"batch": zp}):
        pl.semaphore_signal(barrier, inc=1, device_id=peer, device_id_type=MESH)

    small = [
        pltpu.make_async_copy(cb_hbm, cb_ref, local_sem.at[4]),
        pltpu.make_async_copy(hb_hbm, hb_ref, local_sem.at[5]),
    ]
    loads = [
        pltpu.make_async_copy(fwd_hbm, embed.at[0], local_sem.at[0]),
        pltpu.make_async_copy(rev_hbm, embed.at[1], local_sem.at[1]),
        pltpu.make_async_copy(hw_hbm, headw, local_sem.at[2]),
    ]
    chunks = [
        pltpu.make_async_copy(w_hbm.at[:, pl.ds(m * wide, wide)], wbuf.at[m, pl.ds(0, deep)], local_sem.at[3])
        for m in range(blocks)
    ]
    for copy in small + loads[:2] + chunks + loads[2:]:
        copy.start()
    pl.semaphore_wait(barrier, 5)

    def remote(src, dst, send, recv, peer):
        return pltpu.make_async_remote_copy(
            src_ref=src, dst_ref=dst, send_sem=send, recv_sem=recv, device_id=peer, device_id_type=MESH
        )

    tile = halo.shape[2]

    def halo_copy(k, side, target):
        src = (fwd_hbm, rev_hbm)[k].at[pl.ds(0 if side else rows - tile, tile)]
        return remote(src, halo.at[k, side], halo_send.at[k, side], halo_recv.at[k, side], {"seq": target})

    def cell(slot, color, j):
        row = pl.multiple_of(slot * deep + (j % SPLIT) * part + color * grain, tile)
        return wbuf.at[j // SPLIT, pl.ds(row, grain)]

    def x_copy(j):
        row = pl.ds(pl.multiple_of((j % SPLIT) * part + cx * grain, tile), grain)
        col = pl.ds(pl.multiple_of((j // SPLIT) * wide, wide), wide)
        return remote(w_hbm.at[row, col], cell(2, cx, j), x_send, x_recv.at[j], {"seq": across})

    def y_copy(kind, j):
        ref = cell(2, cz, j).at[:, pl.ds(thin, thin)] if kind else cell(2, cx, j)
        return remote(ref, ref, y_send.at[kind], y_recv.at[kind, j], {"batch": yp})

    def z_copy(kind, j):
        ref = cell(2, cy, j).at[:, pl.ds(0, thin)] if kind else cell(2, cx, j)
        return remote(ref, ref, z_send.at[kind], z_recv.at[kind, j], {"batch": zp})

    def m_copy(color, j):
        return remote(cell(2, color, j), cell(3, color, j), m_send, m_recv.at[j // SPLIT], {"seq": mate})

    def stripe(share):
        return wbuf.at[:, pl.ds(0, deep // share)]

    guests = remote(
        rev_hbm.at[pl.ds(kept - tile, visit + tile)], guest, guest_sem.at[0], guest_sem.at[1], {"seq": mirror}
    )
    own = [
        remote(w_hbm.at[:, pl.ds(m * wide, wide)], wbuf.at[m, pl.ds(deep, deep)], own_send, own_recv, {"seq": mate})
        for m in range(blocks)
    ]

    def start_x(j, c):
        x_copy(j).start()
        return c

    lax.fori_loop(0, SPLIT, start_x, 0)

    @pl.when(s < 3)
    def _():
        halo_copy(0, 0, s + 1).start()
        halo_copy(1, 0, s + 1).start()

    @pl.when(s > 0)
    def _():
        halo_copy(0, 1, s - 1).start()

    @pl.when(core == 1)
    def _():
        halo_copy(1, 1, across).start()

    lax.fori_loop(SPLIT, units, start_x, 0)
    guests.start()
    for copy in own:
        copy.start()

    r = lax.broadcasted_iota(jnp.int32, (rows, rows), 0)
    c = lax.broadcasted_iota(jnp.int32, (rows, rows), 1)
    flip[...] = jnp.where(r + c == rows - 1, 1.0, 0.0).astype(BF16)
    for copy in small:
        copy.wait()
    for k in range(2):
        logits[k] = jnp.broadcast_to(hb_ref[...], (rows, tracks))

    line = lax.broadcasted_iota(jnp.int32, (rows, depth), 0)

    def shard_of(slot):
        return (far + (slot // 2) * (1 - 2 * far)) * 2 + core + (slot % 2) * (1 - 2 * core)

    def build_guest(slot, carry):
        cols = pl.ds(pl.multiple_of(shard_of(slot) * depth, LANES), depth)
        full = guest[:, cols].astype(F32)
        high = halo[1, 1, :, cols].astype(F32)[0:1]
        before = pltpu.roll(full, 1, 0)[tile:]
        after = pltpu.roll(full, visit + tile - 1, 0)[tile:]
        after = jnp.where(lax.broadcasted_iota(jnp.int32, (visit, depth), 0) == visit - 1, high, after)
        for tap, value in enumerate((before, full[tile:], after)):
            place = pl.ds(pl.multiple_of((slot * taps + tap) * depth, LANES), depth)
            xcat[1, pl.ds(kept, visit), place] = value.astype(BF16)
        return carry

    def build(k, slot):
        shard = shard_of(slot)
        cols = pl.ds(pl.multiple_of(shard * depth, LANES), depth)
        mid = embed[k, :, cols]
        wide_mid = mid.astype(F32)
        low = halo[k, 0, :, cols].astype(F32)[tile - 1 : tile]
        high = halo[k, 1, :, cols].astype(F32)[0:1]
        before = jnp.where(line == 0, low, pltpu.roll(wide_mid, 1, 0))
        after = jnp.where(line == rows - 1, high, pltpu.roll(wide_mid, rows - 1, 0))
        for tap, value in enumerate((before.astype(BF16), mid, after.astype(BF16))):
            xcat[k, :, pl.ds(pl.multiple_of((slot * taps + tap) * depth, LANES), depth)] = value

    def near(k, m):
        cols = pl.ds(pl.multiple_of(m * wide, wide), wide)
        own_rows = pl.ds(0, kept if k else rows)
        acc[k, own_rows, cols] = (
            jnp.dot(xcat[k, own_rows, pl.ds(0, half)], wbuf[m, pl.ds(0, half)], preferred_element_type=F32)
            + cb_ref[:, cols]
        )

    def remote_part(k, m):
        cols = pl.ds(pl.multiple_of(m * wide, wide), wide)
        own_rows = pl.ds(0, kept if k else rows)
        total = acc[k, own_rows, cols] + jnp.dot(
            xcat[k, own_rows, pl.ds(half, half)], wbuf[m, pl.ds(half, half)], preferred_element_type=F32
        )
        hidden = gelu(total).astype(BF16)
        logits[k, own_rows] = logits[k, own_rows] + jnp.dot(hidden, headw[cols, :], preferred_element_type=F32)

    def guest_part(m, carry):
        cols = pl.ds(pl.multiple_of(m * wide, wide), wide)
        part_rows = pl.ds(kept, visit)
        total = jnp.dot(xcat[1, part_rows, :], wbuf[m], preferred_element_type=F32) + cb_ref[:, cols]
        hidden = gelu(total).astype(BF16)
        logits[1, part_rows] = logits[1, part_rows] + jnp.dot(hidden, headw[cols, :], preferred_element_type=F32)
        return carry

    def first(i, carry):
        build(i % 2, i // 2)
        return carry

    def step(j, carry):
        @pl.when(j < units)
        def _():
            x_copy(j).wait_recv()
            y_copy(0, j).start()
            z_copy(0, j).start()
            m_copy(cx, j).start()

        @pl.when((j >= LAG) & (j < units + LAG))
        def _():
            y_copy(0, j - LAG).wait_recv()
            z_copy(1, j - LAG).start()
            m_copy(cy, j - LAG).start()
            z_copy(0, j - LAG).wait_recv()
            y_copy(1, j - LAG).start()
            m_copy(cz, j - LAG).start()

        @pl.when((j >= LAG + LAG2) & (j < units + LAG + LAG2))
        def _():
            y_copy(1, j - LAG - LAG2).wait_recv()
            z_copy(1, j - LAG - LAG2).wait_recv()
            m_copy(cd, j - LAG - LAG2).start()

        @pl.when(j == START)
        def _():
            for copy in loads[:2]:
                copy.wait()

            @pl.when(s == 0)
            def _():
                halo[0, 0] = jnp.zeros_like(halo[0, 0])
                halo[1, 0] = jnp.zeros_like(halo[1, 0])
                halo[1, 1] = jnp.zeros_like(halo[1, 1])

            @pl.when(s == 3)
            def _():
                halo[0, 1] = jnp.zeros_like(halo[0, 1])

            @pl.when(s == 2)
            def _():
                halo[1, 1] = embed[1, pl.ds(0, tile)]

            @pl.when(s > 0)
            def _():
                halo_copy(0, 0, mate).wait_recv()
                halo_copy(1, 0, mate).wait_recv()

            @pl.when(s < 3)
            def _():
                halo_copy(0, 1, mate).wait_recv()

            @pl.when(core == 1)
            def _():
                halo_copy(1, 1, across).wait_recv()

            lax.fori_loop(0, 8, first, 0)
            loads[2].wait()
            whole = wbuf.at[:, pl.ds(0, deep)]
            pltpu.make_async_copy(whole, whole, local_sem.at[3]).wait()
            remote(whole, wbuf.at[:, pl.ds(deep, deep)], own_send, own_recv, {"seq": mate}).wait()

        pace = SPLIT // 2

        @pl.when((j > START) & ((j - 1 - START) % pace == 0) & (j < units + 1 + START))
        def _():
            i = (j - 1 - START) // pace

            @pl.when(i % 2 == 0)
            def _():
                near(1, i // 2)

            @pl.when(i % 2 == 1)
            def _():
                near(0, i // 2)

        late = j - SPLIT - LAG - LAG2

        @pl.when((late >= 0) & (late % pace == 0))
        def _():
            k = 1 - late // pace % 2
            m = late // SPLIT

            @pl.when(k == 1)
            def _():
                full = wbuf.at[m, pl.ds(0, deep)]
                remote(full, full, m_send, m_recv.at[m], {"seq": mate}).wait_recv()
                remote_part(1, m)

            @pl.when(k == 0)
            def _():
                remote_part(0, m)

        return carry

    lax.fori_loop(0, units + LAG + LAG2 + 1, step, 0)

    def t_copy(p):
        cols = pl.ds(p * wide, wide)
        return remote(sendt.at[pl.ds(0, kept), cols], rev_out.at[pl.ds(visit, kept), cols], t_send.at[p], t_recv.at[p], {"seq": mirror})

    for p in range(pieces):
        cols = pl.ds(p * wide, wide)
        value = softplus(logits[1, pl.ds(0, kept), cols]).astype(BF16)
        turn = flip[pl.ds(visit, kept), pl.ds(0, kept)]
        sendt[pl.ds(0, kept), cols] = jnp.dot(turn, value, preferred_element_type=F32).astype(BF16)
        if p:
            t_copy(p - 1).start()
    remote_part(0, blocks - 1)
    t_copy(pieces - 1).start()
    keep = []
    for p in range(pieces):
        cols = pl.ds(p * wide, wide)
        keept[:, cols] = softplus(logits[0, :, cols]).astype(BF16)
        keep.append(pltpu.make_async_copy(keept.at[:, cols], fwd_out.at[:, cols], out_sem.at[p]))
        if p:
            keep[p - 1].start()

    guests.wait_recv()
    keep[-1].start()
    lax.fori_loop(0, 4, build_guest, 0)
    lax.fori_loop(0, blocks, guest_part, 0)
    value = softplus(logits[1, pl.ds(kept, visit)]).astype(BF16)
    turn = flip[pl.ds(0, visit), pl.ds(kept, visit)]
    sendt[pl.ds(kept, visit)] = jnp.dot(turn, value, preferred_element_type=F32).astype(BF16)
    keep.append(pltpu.make_async_copy(sendt.at[pl.ds(kept, visit)], rev_out.at[pl.ds(0, visit)], out_sem.at[pieces]))

    remote(stripe(4), stripe(4), x_send, x_recv.at[0], {"seq": across}).wait_send()
    for kind, share in ((0, 4), (1, 8)):
        remote(stripe(share), stripe(share), y_send.at[kind], y_recv.at[kind, 0], {"batch": yp}).wait_send()
        remote(stripe(share), stripe(share), z_send.at[kind], z_recv.at[kind, 0], {"batch": zp}).wait_send()
    remote(stripe(1), stripe(1), m_send, m_recv.at[0], {"seq": mate}).wait_send()

    @pl.when(s < 3)
    def _():
        halo_copy(0, 0, s + 1).wait_send()
        halo_copy(1, 0, s + 1).wait_send()

    @pl.when(s > 0)
    def _():
        halo_copy(0, 1, s - 1).wait_send()

    @pl.when(core == 1)
    def _():
        halo_copy(1, 1, across).wait_send()

    keep[-1].start()
    for copy in keep:
        copy.wait()
    guests.wait_send()
    for p in range(pieces):
        t_copy(p).wait()


def fused(forward_embed, reverse_embed, conv_weight, conv_bias, head_weight, head_bias):
    rows, channels = forward_embed.shape
    _, taps, depth, _ = conv_weight.shape
    tracks = head_weight.shape[1]
    blocks = channels // WIDE
    units = SPLIT * blocks
    pieces = tracks // WIDE
    dma = pltpu.SemaphoreType.DMA
    anywhere = pl.BlockSpec(memory_space=pl.ANY)
    forward_tracks, reverse_tracks = pl.pallas_call(
        functools.partial(kernel, taps),
        out_shape=[jax.ShapeDtypeStruct((rows, tracks), BF16)] * 2,
        in_specs=[anywhere] * 6,
        out_specs=[anywhere, anywhere],
        scratch_shapes=[
            pltpu.VMEM((2, rows, channels), BF16),
            pltpu.VMEM((2, 2, 16, channels), BF16),
            pltpu.VMEM((rows * VISIT // 24 + 16, channels), BF16),
            pltpu.VMEM((2, rows, 4 * taps * depth), BF16),
            pltpu.VMEM((blocks, 4 * taps * depth, WIDE), BF16),
            pltpu.VMEM((2, rows, channels), F32),
            pltpu.VMEM((channels, tracks), BF16),
            pltpu.VMEM((2, rows, tracks), F32),
            pltpu.VMEM((rows, rows), BF16),
            pltpu.VMEM((rows, tracks), BF16),
            pltpu.VMEM((rows, tracks), BF16),
            pltpu.VMEM((1, channels), F32),
            pltpu.VMEM((1, tracks), F32),
            dma((6,)),
            dma((2, 2)), dma((2, 2)),
            dma, dma,
            dma, dma((units,)),
            dma((2,)), dma((2, units)),
            dma((2,)), dma((2, units)),
            dma, dma((blocks,)),
            dma((pieces,)), dma((pieces,)), dma((pieces + 1,)), dma((2,)),
        ],
        compiler_params=pltpu.CompilerParams(
            collective_id=0, has_side_effects=True, vmem_limit_bytes=62 * 1024 * 1024
        ),
    )(forward_embed, reverse_embed, conv_weight.reshape(taps * depth, channels), conv_bias, head_weight, head_bias[None])
    return (0.5 * (forward_tracks.astype(F32) + reverse_tracks.astype(F32))).astype(BF16)


def with_halo(block, axis):
    count = lax.axis_size(axis)
    forward = [(i, i + 1) for i in range(count - 1)]
    backward = [(target, source) for source, target in forward]
    low = lax.ppermute(block[-1:], axis, forward)
    high = lax.ppermute(block[:1], axis, backward)
    return jnp.concatenate([low, block, high], axis=0)


def general(forward_embed, reverse_embed, conv_weight, conv_bias, head_weight, head_bias):
    count = lax.axis_size("seq")
    layers, taps = conv_weight.shape[:2]
    gathered = [lax.all_gather(conv_weight[n], "seq", axis=1, tiled=True) for n in range(layers)]

    def strand(hidden):
        for n in range(layers):
            rows = hidden.shape[0]
            padded = with_halo(hidden, "seq")
            total = sum(
                jnp.dot(padded[k : k + rows], gathered[n][k], preferred_element_type=F32) for k in range(taps)
            )
            hidden = jax.nn.gelu(total + conv_bias[n], approximate=False).astype(BF16)
        logits = jnp.dot(hidden, head_weight, preferred_element_type=F32) + head_bias
        return jax.nn.softplus(logits).astype(BF16)

    reverse_tracks = strand(reverse_embed)[::-1]
    reverse_tracks = lax.ppermute(reverse_tracks, "seq", [(i, count - 1 - i) for i in range(count)])
    mean = 0.5 * (strand(forward_embed).astype(F32) + reverse_tracks.astype(F32))
    return mean.astype(BF16)


def solution(mesh):
    cubes = mesh.shape["seq"] == 4 and mesh.shape["batch"] % 4 == 0
    return jax.shard_map(
        fused if cubes else general,
        mesh=mesh,
        in_specs=(
            P(("batch", "seq"), None),
            P(("batch", "seq"), None),
            P(None, None, "seq", None),
            P(),
            P(),
            P(),
        ),
        out_specs=P(("batch", "seq"), None),
        check_vma=False,
    )
```

```python
import functools
import math

import jax
import jax.numpy as jnp
from jax import lax
from jax.experimental import pallas as pl
from jax.experimental.pallas import tpu as pltpu
from jax.sharding import PartitionSpec as P

MESH = pl.DeviceIdType.MESH
F32 = jnp.float32
BF16 = jnp.bfloat16
LANES = 128
WIDE = 256
SPLIT = 2
PAIR = 2
TILE = 8
START = 2
LAG = 2
LAG2 = 2
COLORS = 4
VISIT = 13


def gelu(x):
    return (0.5 * x) * (1.0 + lax.erf(x * math.sqrt(0.5)))


def softplus(x):
    u = jnp.exp(-jnp.abs(x))
    return jnp.maximum(x, 0.0) + jnp.where(u < 1e-3, u - 0.5 * u * u, jnp.log(1.0 + u))


def kernel(
    taps, fwd_hbm, rev_hbm, w_hbm, cb_hbm, hw_hbm, hb_hbm, fwd_out, rev_out,
    embed, halo, guest, xcat, wbuf, acc, headw, logits, flip, sendt, keept, cb_ref, hb_ref,
    local_sem, halo_send, halo_recv, own_send, own_recv,
    x_send, x_recv, y_send, y_recv, z_send, z_recv, m_send, m_recv, t_send, t_recv, out_sem, guest_sem,
):
    s = lax.axis_index("seq")
    b = lax.axis_index("batch")
    core = s % 2
    far = s // 2
    mate = s + 1 - 2 * core
    across = s + 2 - 4 * far
    mirror = 3 - s
    shards = (s, mate, across, mirror)
    y = b % 2
    z = (b // 2) % 2
    yp = b + 1 - 2 * y
    zp = b + 2 - 4 * z
    cx = 2 * z + y
    cy = 2 * z + 1 - y
    cz = 2 * (1 - z) + y
    cd = 2 * (1 - z) + 1 - y
    rows, channels = embed.shape[1:]
    deep = w_hbm.shape[0]
    depth = deep // taps
    wide = WIDE
    blocks = channels // wide
    units = SPLIT * blocks
    part = deep // SPLIT
    grain = part // COLORS
    thin = wide // 2
    half = 2 * taps * depth
    tracks = hb_ref.shape[1]
    pieces = tracks // wide
    visit = guest.shape[0] - halo.shape[2]
    kept = rows - visit

    barrier = pltpu.get_barrier_semaphore()
    for peer in ({"seq": mate}, {"seq": across}, {"seq": mirror}, {"batch": yp}, {"batch": zp}):
        pl.semaphore_signal(barrier, inc=1, device_id=peer, device_id_type=MESH)

    small = [
        pltpu.make_async_copy(cb_hbm, cb_ref, local_sem.at[4]),
        pltpu.make_async_copy(hb_hbm, hb_ref, local_sem.at[5]),
    ]
    loads = [
        pltpu.make_async_copy(fwd_hbm, embed.at[0], local_sem.at[0]),
        pltpu.make_async_copy(rev_hbm, embed.at[1], local_sem.at[1]),
        pltpu.make_async_copy(hw_hbm, headw, local_sem.at[2]),
    ]
    chunks = [
        pltpu.make_async_copy(w_hbm.at[:, pl.ds(m * wide, wide)], wbuf.at[m, pl.ds(0, deep)], local_sem.at[3])
        for m in range(blocks)
    ]
    for copy in small + loads[:2] + chunks + loads[2:]:
        copy.start()
    pl.semaphore_wait(barrier, 5)

    def remote(src, dst, send, recv, peer):
        return pltpu.make_async_remote_copy(
            src_ref=src, dst_ref=dst, send_sem=send, recv_sem=recv, device_id=peer, device_id_type=MESH
        )

    tile = halo.shape[2]

    def halo_copy(k, side, target):
        src = (fwd_hbm, rev_hbm)[k].at[pl.ds(0 if side else rows - tile, tile)]
        return remote(src, halo.at[k, side], halo_send.at[k, side], halo_recv.at[k, side], {"seq": target})

    def cell(slot, color, j):
        row = pl.multiple_of(slot * deep + (j % SPLIT) * part + color * grain, 16)
        return wbuf.at[j // SPLIT, pl.ds(row, grain)]

    def x_copy(j):
        row = pl.ds(pl.multiple_of((j % SPLIT) * part + cx * grain, 16), grain)
        col = pl.ds(pl.multiple_of((j // SPLIT) * wide, wide), wide)
        return remote(w_hbm.at[row, col], cell(2, cx, j), x_send, x_recv.at[j], {"seq": across})

    def y_copy(kind, j):
        ref = cell(2, cz, j).at[:, pl.ds(thin, thin)] if kind else cell(2, cx, j)
        return remote(ref, ref, y_send.at[kind], y_recv.at[kind, j], {"batch": yp})

    def z_copy(kind, j):
        ref = cell(2, cy, j).at[:, pl.ds(0, thin)] if kind else cell(2, cx, j)
        return remote(ref, ref, z_send.at[kind], z_recv.at[kind, j], {"batch": zp})

    def m_copy(color, j):
        return remote(cell(2, color, j), cell(3, color, j), m_send, m_recv.at[j // SPLIT], {"seq": mate})

    def stripe(share):
        return wbuf.at[:, pl.ds(0, deep // share)]

    guests = remote(
        rev_hbm.at[pl.ds(kept - tile, visit + tile)], guest, guest_sem.at[0], guest_sem.at[1], {"seq": mirror}
    )
    own = [
        remote(w_hbm.at[:, pl.ds(m * wide, wide)], wbuf.at[m, pl.ds(deep, deep)], own_send, own_recv, {"seq": mate})
        for m in range(blocks)
    ]

    def start_x(j, c):
        x_copy(j).start()
        return c

    lax.fori_loop(0, SPLIT, start_x, 0)

    @pl.when(s < 3)
    def _():
        halo_copy(0, 0, s + 1).start()
        halo_copy(1, 0, s + 1).start()

    @pl.when(s > 0)
    def _():
        halo_copy(0, 1, s - 1).start()

    @pl.when(core == 1)
    def _():
        halo_copy(1, 1, across).start()

    lax.fori_loop(SPLIT, units, start_x, 0)
    guests.start()
    for copy in own:
        copy.start()

    r = lax.broadcasted_iota(jnp.int32, (rows, rows), 0)
    c = lax.broadcasted_iota(jnp.int32, (rows, rows), 1)
    flip[...] = jnp.where(r + c == rows - 1, 1.0, 0.0).astype(BF16)
    for copy in small:
        copy.wait()
    for k in range(2):
        logits[k] = jnp.broadcast_to(hb_ref[...], (rows, tracks))

    line = lax.broadcasted_iota(jnp.int32, (rows, depth), 0)

    def shard_of(slot):
        return (far + (slot // 2) * (1 - 2 * far)) * 2 + core + (slot % 2) * (1 - 2 * core)

    def build_guest(slot, carry):
        cols = pl.ds(pl.multiple_of(shard_of(slot) * depth, LANES), depth)
        full = guest[:, cols].astype(F32)
        high = halo[1, 1, :, cols].astype(F32)[0:1]
        before = pltpu.roll(full, 1, 0)[tile:]
        after = pltpu.roll(full, visit + tile - 1, 0)[tile:]
        after = jnp.where(lax.broadcasted_iota(jnp.int32, (visit, depth), 0) == visit - 1, high, after)
        for tap, value in enumerate((before, full[tile:], after)):
            place = pl.ds(pl.multiple_of((slot * taps + tap) * depth, LANES), depth)
            xcat[1, pl.ds(kept, visit), place] = value.astype(BF16)
        return carry

    def build(k, slot):
        shard = shard_of(slot)
        cols = pl.ds(pl.multiple_of(shard * depth, LANES), depth)
        mid = embed[k, :, cols]
        wide_mid = mid.astype(F32)
        low = halo[k, 0, :, cols].astype(F32)[tile - 1 : tile]
        high = halo[k, 1, :, cols].astype(F32)[0:1]
        before = jnp.where(line == 0, low, pltpu.roll(wide_mid, 1, 0))
        after = jnp.where(line == rows - 1, high, pltpu.roll(wide_mid, rows - 1, 0))
        for tap, value in enumerate((before.astype(BF16), mid, after.astype(BF16))):
            xcat[k, :, pl.ds(pl.multiple_of((slot * taps + tap) * depth, LANES), depth)] = value

    def near(k, m):
        cols = pl.ds(pl.multiple_of(m * wide, wide), wide)
        own_rows = pl.ds(0, kept if k else rows)
        acc[k, own_rows, cols] = (
            jnp.dot(xcat[k, own_rows, pl.ds(0, half)], wbuf[m, pl.ds(0, half)], preferred_element_type=F32)
            + cb_ref[:, cols]
        )

    def remote_part(k, m):
        cols = pl.ds(pl.multiple_of(m * wide, wide), wide)
        own_rows = pl.ds(0, kept if k else rows)
        total = acc[k, own_rows, cols] + jnp.dot(
            xcat[k, own_rows, pl.ds(half, half)], wbuf[m, pl.ds(half, half)], preferred_element_type=F32
        )
        hidden = gelu(total).astype(BF16)
        logits[k, own_rows] = logits[k, own_rows] + jnp.dot(hidden, headw[cols, :], preferred_element_type=F32)

    def guest_part(i, carry):
        part_rows = pl.ds(kept, visit)
        hidden = []
        for m in (PAIR * i + n for n in range(PAIR)):
            cols = pl.ds(pl.multiple_of(m * wide, wide), wide)
            total = jnp.dot(xcat[1, part_rows, :], wbuf[m], preferred_element_type=F32) + cb_ref[:, cols]
            hidden.append(gelu(total).astype(BF16))
        span = pl.ds(pl.multiple_of(i * PAIR * wide, wide), PAIR * wide)
        logits[1, part_rows] = logits[1, part_rows] + jnp.dot(
            jnp.concatenate(hidden, axis=1), headw[span, :], preferred_element_type=F32
        )
        return carry

    def first(i, carry):
        build(i % 2, i // 2)
        return carry

    def step(j, carry):
        @pl.when(j < units)
        def _():
            x_copy(j).wait_recv()
            y_copy(0, j).start()
            z_copy(0, j).start()
            m_copy(cx, j).start()

        @pl.when((j >= LAG) & (j < units + LAG))
        def _():
            y_copy(0, j - LAG).wait_recv()
            z_copy(1, j - LAG).start()
            m_copy(cy, j - LAG).start()
            z_copy(0, j - LAG).wait_recv()
            y_copy(1, j - LAG).start()
            m_copy(cz, j - LAG).start()

        @pl.when((j >= LAG + LAG2) & (j < units + LAG + LAG2))
        def _():
            y_copy(1, j - LAG - LAG2).wait_recv()
            z_copy(1, j - LAG - LAG2).wait_recv()
            m_copy(cd, j - LAG - LAG2).start()

        @pl.when(j == START)
        def _():
            for copy in loads[:2]:
                copy.wait()

            @pl.when(s == 0)
            def _():
                halo[0, 0] = jnp.zeros_like(halo[0, 0])
                halo[1, 0] = jnp.zeros_like(halo[1, 0])
                halo[1, 1] = jnp.zeros_like(halo[1, 1])

            @pl.when(s == 3)
            def _():
                halo[0, 1] = jnp.zeros_like(halo[0, 1])

            @pl.when(s == 2)
            def _():
                halo[1, 1] = embed[1, pl.ds(0, tile)]

            @pl.when(s > 0)
            def _():
                halo_copy(0, 0, mate).wait_recv()
                halo_copy(1, 0, mate).wait_recv()

            @pl.when(s < 3)
            def _():
                halo_copy(0, 1, mate).wait_recv()

            @pl.when(core == 1)
            def _():
                halo_copy(1, 1, across).wait_recv()

            lax.fori_loop(0, 8, first, 0)
            loads[2].wait()
            whole = wbuf.at[:, pl.ds(0, deep)]
            pltpu.make_async_copy(whole, whole, local_sem.at[3]).wait()
            remote(whole, wbuf.at[:, pl.ds(deep, deep)], own_send, own_recv, {"seq": mate}).wait()

        pace = SPLIT // 2

        @pl.when((j > START) & ((j - 1 - START) % pace == 0) & (j < units + 1 + START))
        def _():
            i = (j - 1 - START) // pace

            @pl.when(i % 2 == 0)
            def _():
                near(1, i // 2)

            @pl.when(i % 2 == 1)
            def _():
                near(0, i // 2)

        late = j - SPLIT - LAG - LAG2

        @pl.when((late >= 0) & (late % pace == 0))
        def _():
            k = 1 - late // pace % 2
            m = late // SPLIT

            @pl.when(k == 1)
            def _():
                full = wbuf.at[m, pl.ds(0, deep)]
                remote(full, full, m_send, m_recv.at[m], {"seq": mate}).wait_recv()
                remote_part(1, m)

            @pl.when(k == 0)
            def _():
                remote_part(0, m)

        return carry

    lax.fori_loop(0, units + LAG + LAG2 + 1, step, 0)

    def t_copy(p):
        cols = pl.ds(p * wide, wide)
        return remote(sendt.at[pl.ds(0, kept), cols], rev_out.at[pl.ds(visit, kept), cols], t_send.at[p], t_recv.at[p], {"seq": mirror})

    for p in range(pieces):
        cols = pl.ds(p * wide, wide)
        value = softplus(logits[1, pl.ds(0, kept), cols]).astype(BF16)
        turn = flip[pl.ds(visit, kept), pl.ds(0, kept)]
        sendt[pl.ds(0, kept), cols] = jnp.dot(turn, value, preferred_element_type=F32).astype(BF16)
        if p:
            t_copy(p - 1).start()
    remote_part(0, blocks - 1)
    t_copy(pieces - 1).start()
    keep = []
    for p in range(pieces):
        cols = pl.ds(p * wide, wide)
        keept[:, cols] = softplus(logits[0, :, cols]).astype(BF16)
        keep.append(pltpu.make_async_copy(keept.at[:, cols], fwd_out.at[:, cols], out_sem.at[p]))
        if p:
            keep[p - 1].start()

    guests.wait_recv()
    keep[-1].start()
    lax.fori_loop(0, 4, build_guest, 0)
    lax.fori_loop(0, blocks // PAIR, guest_part, 0)
    value = softplus(logits[1, pl.ds(kept, visit)]).astype(BF16)
    turn = flip[pl.ds(0, visit), pl.ds(kept, visit)]
    sendt[pl.ds(kept, visit)] = jnp.dot(turn, value, preferred_element_type=F32).astype(BF16)
    keep.append(pltpu.make_async_copy(sendt.at[pl.ds(kept, visit)], rev_out.at[pl.ds(0, visit)], out_sem.at[pieces]))

    remote(stripe(4), stripe(4), x_send, x_recv.at[0], {"seq": across}).wait_send()
    for kind, share in ((0, 4), (1, 8)):
        remote(stripe(share), stripe(share), y_send.at[kind], y_recv.at[kind, 0], {"batch": yp}).wait_send()
        remote(stripe(share), stripe(share), z_send.at[kind], z_recv.at[kind, 0], {"batch": zp}).wait_send()
    remote(stripe(1), stripe(1), m_send, m_recv.at[0], {"seq": mate}).wait_send()

    @pl.when(s < 3)
    def _():
        halo_copy(0, 0, s + 1).wait_send()
        halo_copy(1, 0, s + 1).wait_send()

    @pl.when(s > 0)
    def _():
        halo_copy(0, 1, s - 1).wait_send()

    @pl.when(core == 1)
    def _():
        halo_copy(1, 1, across).wait_send()

    keep[-1].start()
    for copy in keep:
        copy.wait()
    guests.wait_send()
    for p in range(pieces):
        t_copy(p).wait()


def fused(forward_embed, reverse_embed, conv_weight, conv_bias, head_weight, head_bias):
    rows, channels = forward_embed.shape
    _, taps, depth, _ = conv_weight.shape
    tracks = head_weight.shape[1]
    blocks = channels // WIDE
    units = SPLIT * blocks
    pieces = tracks // WIDE
    dma = pltpu.SemaphoreType.DMA
    anywhere = pl.BlockSpec(memory_space=pl.ANY)
    forward_tracks, reverse_tracks = pl.pallas_call(
        functools.partial(kernel, taps),
        out_shape=[jax.ShapeDtypeStruct((rows, tracks), BF16)] * 2,
        in_specs=[anywhere] * 6,
        out_specs=[anywhere, anywhere],
        scratch_shapes=[
            pltpu.VMEM((2, rows, channels), BF16),
            pltpu.VMEM((2, 2, TILE, channels), BF16),
            pltpu.VMEM((rows * VISIT // 24 + TILE, channels), BF16),
            pltpu.VMEM((2, rows, 4 * taps * depth), BF16),
            pltpu.VMEM((blocks, 4 * taps * depth, WIDE), BF16),
            pltpu.VMEM((2, rows, channels), F32),
            pltpu.VMEM((channels, tracks), BF16),
            pltpu.VMEM((2, rows, tracks), F32),
            pltpu.VMEM((rows, rows), BF16),
            pltpu.VMEM((rows, tracks), BF16),
            pltpu.VMEM((rows, tracks), BF16),
            pltpu.VMEM((1, channels), F32),
            pltpu.VMEM((1, tracks), F32),
            dma((6,)),
            dma((2, 2)), dma((2, 2)),
            dma, dma,
            dma, dma((units,)),
            dma((2,)), dma((2, units)),
            dma((2,)), dma((2, units)),
            dma, dma((blocks,)),
            dma((pieces,)), dma((pieces,)), dma((pieces + 1,)), dma((2,)),
        ],
        compiler_params=pltpu.CompilerParams(
            collective_id=0, has_side_effects=True, vmem_limit_bytes=62 * 1024 * 1024
        ),
    )(forward_embed, reverse_embed, conv_weight.reshape(taps * depth, channels), conv_bias, head_weight, head_bias[None])
    return (0.5 * (forward_tracks.astype(F32) + reverse_tracks.astype(F32))).astype(BF16)


def with_halo(block, axis):
    count = lax.axis_size(axis)
    forward = [(i, i + 1) for i in range(count - 1)]
    backward = [(target, source) for source, target in forward]
    low = lax.ppermute(block[-1:], axis, forward)
    high = lax.ppermute(block[:1], axis, backward)
    return jnp.concatenate([low, block, high], axis=0)


def general(forward_embed, reverse_embed, conv_weight, conv_bias, head_weight, head_bias):
    count = lax.axis_size("seq")
    layers, taps = conv_weight.shape[:2]
    gathered = [lax.all_gather(conv_weight[n], "seq", axis=1, tiled=True) for n in range(layers)]

    def strand(hidden):
        for n in range(layers):
            rows = hidden.shape[0]
            padded = with_halo(hidden, "seq")
            total = sum(
                jnp.dot(padded[k : k + rows], gathered[n][k], preferred_element_type=F32) for k in range(taps)
            )
            hidden = jax.nn.gelu(total + conv_bias[n], approximate=False).astype(BF16)
        logits = jnp.dot(hidden, head_weight, preferred_element_type=F32) + head_bias
        return jax.nn.softplus(logits).astype(BF16)

    reverse_tracks = strand(reverse_embed)[::-1]
    reverse_tracks = lax.ppermute(reverse_tracks, "seq", [(i, count - 1 - i) for i in range(count)])
    mean = 0.5 * (strand(forward_embed).astype(F32) + reverse_tracks.astype(F32))
    return mean.astype(BF16)


def solution(mesh):
    cubes = mesh.shape["seq"] == 4 and mesh.shape["batch"] % 4 == 0
    return jax.shard_map(
        fused if cubes else general,
        mesh=mesh,
        in_specs=(
            P(("batch", "seq"), None),
            P(("batch", "seq"), None),
            P(None, None, "seq", None),
            P(),
            P(),
            P(),
        ),
        out_specs=P(("batch", "seq"), None),
        check_vma=False,
    )
```
